32 devices in a mesh: grp: 8 (over y, x, core), tp: 4 (over z).
Axes of the slice: x: 2, y: 2, z: 4, core: 2. Of those that a mesh axis runs over, the one named last changes fastest.
Arguments:
- text_embeds: bfloat16 [16384, 8192], P('grp', 'tp'), may hold values from -6 to 6
- image_embeds: bfloat16 [8192, 8192], P(('grp', 'tp')), may hold values from -6 to 6
- image_offsets: int32 [16, 2], P('grp'), may hold values from 0 to 768, as said below
- image_counts: int32 [16], P('grp'), may hold values from 1 to 2
- seq_lengths: int32 [16], P('grp'), may hold values from 513 to 1024
- norm_gain: bfloat16 [8192], P('tp'), may hold values from 0.25 to 1.75
- key_weight: bfloat16 [8192, 512], P('tp'), may hold values from -0.0625 to 0.0625
- key_bias: bfloat16 [512], replicated, may hold values from -3 to 3
- key_cotangent: bfloat16 [16384, 512], P(('grp', 'tp')), may hold values from -0.017944336 to 0.017944336
Outputs:
- key_states: bfloat16 [16384, 512], P(('grp', 'tp'))
- weight_grad: float32 [8192, 512], P('tp')
- bias_grad: float32 [512], replicated
- gain_grad: float32 [8192], P('tp')
The draws below stay inside these ranges and needn't reach their ends.
Inputs may be any that keep to these rules, and one draw needn't show every extreme that they name: `image_offsets`: each sequence's first image_counts slots hold increasing starts of non-intersecting runs of 256 rows that end within its used rows; later slots hold 0.
All inputs are finite; a program needn't handle non-finite values.
Results may differ from the reference program's by a relative error of at most 0.0046.
Values may be sent and summed in bfloat16 or wider, within the bound.
A program may use at most 64 MiB of HBM per device.

```python
import jax
import jax.numpy as jnp
from jax import lax

D = 8192
PATCH_TOK = 256
MAX_IMG = 2
SEQS = 2
LEN = 1024
KEYS = 512
GROUP_ROWS = 2048
IMG_ROWS = 1024
SEQ_TOTAL = 16
TOKENS = 16384
IMG_TOTAL = 8192
N_GRP = 8


def image_layout(key):
    base = jax.random.fold_in(key, 11)
    first_key, second_key, third_key = jax.random.split(base, 3)
    counts = jax.random.randint(first_key, (SEQ_TOTAL,), 1, MAX_IMG + 1).astype(jnp.int32)
    counts = counts.at[0].set(MAX_IMG)
    lengths = jax.random.randint(second_key, (SEQ_TOTAL,), MAX_IMG * PATCH_TOK + 1, LEN + 1).astype(jnp.int32)
    lengths = lengths.at[1].set(LEN)
    spare = lengths - counts * PATCH_TOK
    slot_ids = jnp.arange(MAX_IMG, dtype=jnp.int32)
    starts = jax.random.randint(third_key, (SEQ_TOTAL, MAX_IMG), 0, spare[:, None] + 1).astype(jnp.int32)
    starts = jnp.where(slot_ids[None, :] < counts[:, None], starts, spare[:, None])
    starts = jnp.sort(starts, axis=1)
    offsets = starts + slot_ids[None, :] * PATCH_TOK
    offsets = jnp.where(slot_ids[None, :] < counts[:, None], offsets, 0).astype(jnp.int32)
    return (offsets, counts, lengths)


def draw_image_offsets(key, part):
    return image_layout(key)[0]


def draw_image_counts(key, part):
    return image_layout(key)[1]


def draw_seq_lengths(key, part):
    return image_layout(key)[2]


def levels(own_key, shape, cuts, low, high):
    factor_of, own = 1.0, jax.random.fold_in(own_key, 6)
    for axis_at, shards_of in cuts:
        heights = jnp.exp(jax.random.uniform(jax.random.fold_in(own, axis_at), (shards_of,), jnp.float32, low / len(cuts), high / len(cuts)))
        factor_of = factor_of * jnp.repeat(heights, shape[axis_at] // shards_of).reshape([-1 if axis == axis_at else 1 for axis in range(len(shape))])
    return factor_of


def scatter_about(own_key, shape, scale, most, cuts=(), kind=jnp.bfloat16):
    level = levels(own_key, shape, cuts, -0.22, 0.18) if cuts else 1.0
    drawn = jax.random.normal(own_key, shape, jnp.float32) * scale * level
    return jnp.minimum(jnp.maximum(drawn, -most), most).astype(kind)


def setup_inputs(seed: int = 0) -> dict:
    keys = jax.random.split(jax.random.key(seed), 10)
    return {
        "text_embeds": scatter_about(keys[0], (TOKENS, D), 1.0, 6.0, ((0, 8), (1, 4))),
        "image_embeds": scatter_about(keys[1], (IMG_TOTAL, D), 1.0, 6.0, ((0, 32),)),
        "image_offsets": draw_image_offsets(jax.random.fold_in(keys[9], 71), 0),
        "image_counts": draw_image_counts(jax.random.fold_in(keys[9], 71), 0),
        "seq_lengths": draw_seq_lengths(jax.random.fold_in(keys[9], 71), 0),
        "norm_gain": jnp.clip(1.0 + 0.15 * jax.random.normal(keys[5], (D,), jnp.float32), 0.25, 1.75).astype(jnp.bfloat16),
        "key_weight": scatter_about(keys[6], (D, KEYS), D ** -0.5, 0.0625, ((0, 4),)),
        "key_bias": scatter_about(keys[7], (KEYS,), 0.5, 3.0),
        "key_cotangent": scatter_about(keys[8], (TOKENS, KEYS), 0.003, 0.017944336, ((0, 32),)),
    }


def place_images(text_rows, image_rows, offsets, counts, lengths):
    total_rows = text_rows.shape[0]
    row_ids = jnp.arange(total_rows, dtype=jnp.int32)
    seq_ids = row_ids // LEN
    position = row_ids % LEN
    seq_hot = (seq_ids[:, None] == jnp.arange(offsets.shape[0], dtype=jnp.int32)[None, :]).astype(jnp.int32)
    row_offsets = lax.optimization_barrier(jnp.sum(seq_hot[:, :, None] * offsets[None, :, :], axis=1))
    row_counts = lax.optimization_barrier(jnp.sum(seq_hot * counts[None, :], axis=1))
    row_lengths = lax.optimization_barrier(jnp.sum(seq_hot * lengths[None, :], axis=1))
    slot_ids = jnp.arange(MAX_IMG, dtype=jnp.int32)
    inside = (slot_ids[None, :] < row_counts[:, None]) & (position[:, None] >= row_offsets) & (position[:, None] < row_offsets + PATCH_TOK)
    inside_int = inside.astype(jnp.int32)
    any_inside = lax.optimization_barrier(jnp.sum(inside_int, axis=1)) > 0
    chosen_slot = lax.optimization_barrier(jnp.sum(inside_int * slot_ids[None, :], axis=1))
    chosen_start = lax.optimization_barrier(jnp.sum(inside_int * row_offsets, axis=1))
    source = (seq_ids * MAX_IMG + chosen_slot) * PATCH_TOK + position - chosen_start
    source = jnp.where(any_inside, source, 0).astype(jnp.int32)
    picked = jnp.take(image_rows, source, axis=0)
    merged = jnp.where(any_inside[:, None], picked, text_rows)
    row_valid = (position < row_lengths).astype(jnp.float32)
    return (merged, row_valid)

def reference(text_embeds, image_embeds, image_offsets, image_counts, seq_lengths, norm_gain, key_weight, key_bias, key_cotangent):
    text_groups = text_embeds.reshape(N_GRP, GROUP_ROWS, D)
    image_groups = image_embeds.reshape(N_GRP, IMG_ROWS, D)
    offset_groups = image_offsets.reshape(N_GRP, SEQS, MAX_IMG)
    count_groups = image_counts.reshape(N_GRP, SEQS)
    length_groups = seq_lengths.reshape(N_GRP, SEQS)
    grad_groups = key_cotangent.reshape(N_GRP, GROUP_ROWS, KEYS)
    gain32 = norm_gain.astype(jnp.float32)
    bias32 = key_bias.astype(jnp.float32)

    def one_group(totals, inputs):
        text_rows, image_rows, offsets, counts, lengths, cot_rows = inputs
        merged, row_valid = place_images(text_rows, image_rows, offsets, counts, lengths)
        merged32 = merged.astype(jnp.float32)
        rstd = lax.rsqrt(lax.optimization_barrier(jnp.mean(merged32 * merged32, axis=1)) + 1e-06)
        normed = (merged32 * rstd[:, None] * gain32[None, :]).astype(jnp.bfloat16)
        projected = jnp.dot(normed, key_weight, preferred_element_type=jnp.float32)
        keys_here = ((projected + bias32[None, :]) * row_valid[:, None]).astype(jnp.bfloat16)
        masked_grad = (cot_rows.astype(jnp.float32) * row_valid[:, None]).astype(jnp.bfloat16)
        weight_part = lax.dot_general(normed, masked_grad, (((0,), (0,)), ((), ())), preferred_element_type=jnp.float32)
        bias_part = lax.optimization_barrier(jnp.sum(masked_grad.astype(jnp.float32), axis=0))
        grad_normed = lax.dot_general(masked_grad, key_weight, (((1,), (1,)), ((), ())), preferred_element_type=jnp.float32)
        gain_part = lax.optimization_barrier(jnp.sum(grad_normed * merged32 * rstd[:, None], axis=0))
        return ((totals[0] + weight_part, totals[1] + bias_part, totals[2] + gain_part), keys_here)
    start_totals = (jnp.zeros((D, KEYS), jnp.float32), jnp.zeros((KEYS,), jnp.float32), jnp.zeros((D,), jnp.float32))
    totals, key_groups = lax.scan(one_group, start_totals, (text_groups, image_groups, offset_groups, count_groups, length_groups, grad_groups))
    return (key_groups.reshape(TOKENS, KEYS), totals[0], totals[1], totals[2])
```

```python
import jax
import jax.numpy as jnp
from jax import lax
from jax.sharding import PartitionSpec as P

EPS = 1e-06
F32 = jnp.float32
BF16 = jnp.bfloat16


def on_device(
    text_embeds,
    image_embeds,
    image_offsets,
    image_counts,
    seq_lengths,
    norm_gain,
    key_weight,
    key_bias,
    key_cotangent,
):
    n_tp = lax.axis_size("tp")
    me = lax.axis_index("tp")
    rows = text_embeds.shape[0]
    width = image_embeds.shape[1]
    seqs, slots = image_offsets.shape
    length = rows // seqs
    own_image = image_embeds.shape[0]
    image_total = own_image * n_tp
    patch = image_total // (seqs * slots)
    own_count = key_cotangent.shape[0]

    image_rows = lax.all_to_all(image_embeds, "tp", split_axis=1, concat_axis=0, tiled=True)

    position = lax.broadcasted_iota(jnp.int32, (seqs, length), 1)
    row_valid = (position < seq_lengths[:, None]).astype(F32).reshape(rows)
    own_valid = lax.dynamic_slice_in_dim(row_valid, me * own_count, own_count, 0)
    own_grad = lax.optimization_barrier(
        (key_cotangent.astype(F32) * own_valid[:, None]).astype(BF16)
    )
    masked_grad = lax.all_gather(own_grad, "tp", axis=0, tiled=True)
    bias_grad = lax.psum(jnp.sum(own_grad.astype(F32), axis=0), ("grp", "tp"))

    text32 = text_embeds.astype(F32)
    image32 = image_embeds.astype(F32)
    image_squares = lax.dynamic_update_slice_in_dim(
        jnp.zeros((image_total,), F32), jnp.sum(image32 * image32, axis=1), me * own_image, 0
    )
    squares = lax.psum(
        jnp.concatenate([jnp.sum(text32 * text32, axis=1), image_squares]), "tp"
    )
    rstd = lax.rsqrt(squares / width + EPS)

    slot_used = lax.broadcasted_iota(jnp.int32, (seqs, slots), 1) < image_counts[:, None]
    inside = jnp.zeros((seqs, length), jnp.bool_)
    source = jnp.zeros((seqs, length), jnp.int32)
    first = lax.broadcasted_iota(jnp.int32, (seqs, length), 0) * (slots * patch)
    for k in range(slots):
        start = image_offsets[:, k : k + 1]
        here = slot_used[:, k : k + 1] & (position >= start) & (position < start + patch)
        source = jnp.where(here, first + k * patch + position - start, source)
        inside = inside | here
    text_rstd = rstd[:rows] * (1.0 - inside.astype(F32).reshape(rows))
    image_rstd = rstd[rows:]
    used = jnp.repeat(slot_used.reshape(-1).astype(F32), patch)

    gain32 = norm_gain.astype(F32)
    scaled_weight = (key_weight.astype(F32) * gain32[:, None]).astype(BF16)
    partial = (
        jnp.dot(text_embeds, scaled_weight, preferred_element_type=F32) * text_rstd[:, None]
    ).astype(BF16)
    text_grad = (masked_grad.astype(F32) * text_rstd[:, None]).astype(BF16)
    slot_starts = (
        lax.broadcasted_iota(jnp.int32, (seqs, slots), 0) * length + image_offsets
    ).reshape(-1)
    image_at = (
        slot_starts[:, None] + lax.broadcasted_iota(jnp.int32, (seqs * slots, patch), 1)
    ).reshape(-1)
    picked = jnp.take(masked_grad, image_at, axis=0, mode="clip")
    image_grad = (picked.astype(F32) * (image_rstd * used)[:, None]).astype(BF16)
    over_rows = (((0,), (0,)), ((), ()))
    text_part = lax.dot_general(text_embeds, text_grad, over_rows, preferred_element_type=F32)

    image_keys = (
        jnp.dot(image_rows, scaled_weight, preferred_element_type=F32) * image_rstd[:, None]
    ).astype(BF16)
    placed = jnp.take(image_keys, source.reshape(rows), axis=0, mode="clip")
    partial = jnp.where(inside.reshape(rows)[:, None], placed, partial)
    partial, masked_grad, bias_grad = lax.optimization_barrier((partial, masked_grad, bias_grad))
    projected = lax.psum_scatter(partial, "tp", scatter_dimension=0, tiled=True)
    key_states = (
        (projected.astype(F32) + key_bias.astype(F32)[None, :]) * own_valid[:, None]
    ).astype(BF16)

    image_part = lax.dot_general(image_rows, image_grad, over_rows, preferred_element_type=F32)
    total = lax.psum((text_part + image_part).astype(BF16), "grp").astype(F32)
    weight_grad = total * gain32[:, None]
    gain_grad = jnp.sum(total * key_weight.astype(F32), axis=1)
    return (key_states, weight_grad, bias_grad, gain_grad)


def solution(mesh):
    placed = (
        P("grp", "tp"),
        P(("grp", "tp"), None),
        P("grp", None),
        P("grp"),
        P("grp"),
        P("tp"),
        P("tp", None),
        P(),
        P(("grp", "tp"), None),
    )
    return jax.shard_map(
        on_device,
        mesh=mesh,
        in_specs=placed,
        out_specs=(P(("grp", "tp"), None), P("tp", None), P(), P("tp")),
        check_vma=False,
    )
```

```python
import functools

import jax
import jax.numpy as jnp
from jax import lax
from jax.experimental import pallas as pl
from jax.experimental.pallas import tpu as pltpu
from jax.sharding import PartitionSpec as P

EPS = 1e-06
F32 = jnp.float32
BF16 = jnp.bfloat16


def reduce_kernel(
    n_grp,
    n_tp,
    keys_ref,
    weight_ref,
    bias_ref,
    keys_out,
    weight_out,
    bias_out,
    keys_buf,
    weight_buf,
    bias_buf,
    chunk_buf,
    full_buf,
    keys_send,
    keys_recv,
    weight_send,
    weight_recv,
    bias_send,
    bias_recv,
    full_send,
    full_recv,
):
    g = lax.axis_index("grp")
    t = lax.axis_index("tp")
    own = keys_out.shape[0]
    chunk = chunk_buf.shape[0]

    barrier = pltpu.get_barrier_semaphore()
    for d in range(1, n_grp):
        pl.semaphore_signal(barrier, inc=1, device_id={"grp": lax.rem(g + d, n_grp)})
    for d in range(1, n_tp):
        pl.semaphore_signal(barrier, inc=1, device_id={"tp": lax.rem(t + d, n_tp)})
    pl.semaphore_wait(barrier, n_grp + n_tp - 2)

    def rows_of(index, size):
        return pl.ds(pl.multiple_of(index * size, size), size)

    keys_copies, weight_copies, bias_copies, full_copies = [], [], [], []
    for d in range(1, n_grp):
        peer = lax.rem(g + d, n_grp)
        copy = pltpu.make_async_remote_copy(
            src_ref=weight_ref.at[rows_of(peer, chunk)],
            dst_ref=weight_buf.at[d - 1],
            send_sem=weight_send.at[d - 1],
            recv_sem=weight_recv.at[d - 1],
            device_id={"grp": peer},
        )
        copy.start()
        weight_copies.append(copy)
    for d in range(n_tp - 1, 0, -1):
        peer = lax.rem(t + d, n_tp)
        copy = pltpu.make_async_remote_copy(
            src_ref=keys_ref.at[rows_of(peer, own)],
            dst_ref=keys_buf.at[d - 1],
            send_sem=keys_send.at[d - 1],
            recv_sem=keys_recv.at[d - 1],
            device_id={"tp": peer},
        )
        copy.start()
        keys_copies.append(copy)
    for d in range(1, n_grp):
        copy = pltpu.make_async_remote_copy(
            src_ref=bias_ref,
            dst_ref=bias_buf.at[d - 1],
            send_sem=bias_send.at[d - 1],
            recv_sem=bias_recv.at[d - 1],
            device_id={"grp": lax.rem(g + d, n_grp)},
        )
        copy.start()
        bias_copies.append(copy)

    for copy in weight_copies:
        copy.wait()
    total = weight_ref[rows_of(g, chunk)].astype(F32)
    for d in range(n_grp - 1):
        total = total + weight_buf[d].astype(F32)
    chunk_buf[...] = total.astype(BF16)
    for d in range(1, n_grp):
        copy = pltpu.make_async_remote_copy(
            src_ref=chunk_buf,
            dst_ref=full_buf.at[g],
            send_sem=full_send.at[d - 1],
            recv_sem=full_recv.at[d - 1],
            device_id={"grp": lax.rem(g + d, n_grp)},
        )
        copy.start()
        full_copies.append(copy)
    full_buf[g] = chunk_buf[...]

    for copy in bias_copies:
        copy.wait()
    total = bias_ref[...]
    for d in range(n_grp - 1):
        total = total + bias_buf[d]
    bias_out[...] = total

    for copy in keys_copies:
        copy.wait()
    total = keys_ref[rows_of(t, own)].astype(F32)
    for d in range(n_tp - 1):
        total = total + keys_buf[d].astype(F32)
    keys_out[...] = total

    for copy in full_copies:
        copy.wait()
    weight_out[...] = full_buf[...].reshape(weight_out.shape)


def reduce_all(n_grp, n_tp, keys, weight, bias):
    own = keys.shape[0] // n_tp
    chunk = weight.shape[0] // n_grp
    columns = keys.shape[1]
    vmem = pl.BlockSpec(memory_space=pltpu.VMEM)
    dma = pltpu.SemaphoreType.DMA
    return pl.pallas_call(
        functools.partial(reduce_kernel, n_grp, n_tp),
        out_shape=(
            jax.ShapeDtypeStruct((own, columns), F32),
            jax.ShapeDtypeStruct(weight.shape, BF16),
            jax.ShapeDtypeStruct(bias.shape, F32),
        ),
        in_specs=[vmem] * 3,
        out_specs=(vmem,) * 3,
        scratch_shapes=[
            pltpu.VMEM((n_tp - 1, own, columns), BF16),
            pltpu.VMEM((n_grp - 1, chunk, columns), BF16),
            pltpu.VMEM((n_grp - 1,) + bias.shape, F32),
            pltpu.VMEM((chunk, columns), BF16),
            pltpu.VMEM((n_grp, chunk, columns), BF16),
            dma((n_tp - 1,)),
            dma((n_tp - 1,)),
            dma((n_grp - 1,)),
            dma((n_grp - 1,)),
            dma((n_grp - 1,)),
            dma((n_grp - 1,)),
            dma((n_grp - 1,)),
            dma((n_grp - 1,)),
        ],
        compiler_params=pltpu.CompilerParams(
            collective_id=0, has_side_effects=True, vmem_limit_bytes=32 * 1024 * 1024
        ),
    )(keys, weight, bias)


def on_device(
    text_embeds,
    image_embeds,
    image_offsets,
    image_counts,
    seq_lengths,
    norm_gain,
    key_weight,
    key_bias,
    key_cotangent,
):
    n_tp = lax.axis_size("tp")
    me = lax.axis_index("tp")
    rows = text_embeds.shape[0]
    width = image_embeds.shape[1]
    seqs, slots = image_offsets.shape
    length = rows // seqs
    own_image = image_embeds.shape[0]
    image_total = own_image * n_tp
    patch = image_total // (seqs * slots)
    own_count = key_cotangent.shape[0]

    position = lax.broadcasted_iota(jnp.int32, (seqs, length), 1)
    row_valid = (position < seq_lengths[:, None]).astype(F32).reshape(rows)
    own_valid = lax.dynamic_slice_in_dim(row_valid, me * own_count, own_count, 0)
    own_grad = lax.optimization_barrier(
        (key_cotangent.astype(F32) * own_valid[:, None]).astype(BF16)
    )
    masked_grad = lax.all_gather(own_grad, "tp", axis=0, tiled=True)

    text32 = text_embeds.astype(F32)
    image32 = image_embeds.astype(F32)
    image_squares = lax.dynamic_update_slice_in_dim(
        jnp.zeros((image_total,), F32), jnp.sum(image32 * image32, axis=1), me * own_image, 0
    )
    squares = lax.psum(
        jnp.concatenate([jnp.sum(text32 * text32, axis=1), image_squares]), "tp"
    )
    squares, image_embeds = lax.optimization_barrier((squares, image_embeds))
    blocks = image_embeds.reshape(own_image, n_tp, -1).transpose(1, 0, 2)
    image_rows = lax.all_to_all(blocks, "tp", split_axis=0, concat_axis=0, tiled=True)
    image_rows = image_rows.reshape(image_total, -1)
    rstd = lax.rsqrt(squares / width + EPS)

    slot_used = lax.broadcasted_iota(jnp.int32, (seqs, slots), 1) < image_counts[:, None]
    inside = jnp.zeros((seqs, length), jnp.bool_)
    source = jnp.zeros((seqs, length), jnp.int32)
    first = lax.broadcasted_iota(jnp.int32, (seqs, length), 0) * (slots * patch)
    for k in range(slots):
        start = image_offsets[:, k : k + 1]
        here = slot_used[:, k : k + 1] & (position >= start) & (position < start + patch)
        source = jnp.where(here, first + k * patch + position - start, source)
        inside = inside | here
    text_rstd = rstd[:rows] * (1.0 - inside.astype(F32).reshape(rows))
    image_rstd = rstd[rows:]
    used = jnp.repeat(slot_used.reshape(-1).astype(F32), patch)

    gain32 = norm_gain.astype(F32)
    scaled_weight = (key_weight.astype(F32) * gain32[:, None]).astype(BF16)
    partial = (
        jnp.dot(text_embeds, scaled_weight, preferred_element_type=F32) * text_rstd[:, None]
    ).astype(BF16)
    text_grad = (masked_grad.astype(F32) * text_rstd[:, None]).astype(BF16)
    slot_starts = (
        lax.broadcasted_iota(jnp.int32, (seqs, slots), 0) * length + image_offsets
    ).reshape(-1)
    image_at = (
        slot_starts[:, None] + lax.broadcasted_iota(jnp.int32, (seqs * slots, patch), 1)
    ).reshape(-1)
    picked = jnp.take(masked_grad, image_at, axis=0, mode="clip")
    image_grad = (picked.astype(F32) * (image_rstd * used)[:, None]).astype(BF16)
    over_rows = (((0,), (0,)), ((), ()))
    text_part = lax.dot_general(text_embeds, text_grad, over_rows, preferred_element_type=F32)

    image_rows, partial, text_part, image_grad = lax.optimization_barrier(
        (image_rows, partial, text_part, image_grad)
    )
    image_keys = (
        jnp.dot(image_rows, scaled_weight, preferred_element_type=F32) * image_rstd[:, None]
    ).astype(BF16)
    placed = jnp.take(image_keys, source.reshape(rows), axis=0, mode="clip")
    partial = jnp.where(inside.reshape(rows)[:, None], placed, partial)
    image_part = lax.dot_general(image_rows, image_grad, over_rows, preferred_element_type=F32)
    weight_part = (text_part + image_part).astype(BF16)
    bias_part = jnp.sum(masked_grad.astype(F32).reshape(rows // 8, 8, -1), axis=0)
    n_grp = lax.axis_size("grp")
    if weight_part.shape[0] % (n_grp * 16) == 0 and own_count % 16 == 0:
        projected, total, bias_sum = reduce_all(n_grp, n_tp, partial, weight_part, bias_part)
    else:
        projected = lax.psum_scatter(partial, "tp", scatter_dimension=0, tiled=True)
        total = lax.psum(weight_part, "grp")
        bias_sum = lax.psum(bias_part, "grp")
    key_states = (
        (projected.astype(F32) + key_bias.astype(F32)[None, :]) * own_valid[:, None]
    ).astype(BF16)
    bias_grad = jnp.sum(bias_sum, axis=0)
    total = total.astype(F32)
    weight_grad = total * gain32[:, None]
    gain_grad = jnp.sum(total * key_weight.astype(F32), axis=1)
    return (key_states, weight_grad, bias_grad, gain_grad)


def solution(mesh):
    placed = (
        P("grp", "tp"),
        P(("grp", "tp"), None),
        P("grp", None),
        P("grp"),
        P("grp"),
        P("tp"),
        P("tp", None),
        P(),
        P(("grp", "tp"), None),
    )
    return jax.shard_map(
        on_device,
        mesh=mesh,
        in_specs=placed,
        out_specs=(P(("grp", "tp"), None), P("tp", None), P(), P("tp")),
        check_vma=False,
    )
```

```python
import functools

import jax
import jax.numpy as jnp
from jax import lax
from jax.experimental import pallas as pl
from jax.experimental.pallas import tpu as pltpu
from jax.experimental.layout import Layout, with_layout_constraint
from jax.sharding import PartitionSpec as P

EPS = 1e-06
F32 = jnp.float32
BF16 = jnp.bfloat16


def reduce_kernel(
    n_grp,
    n_tp,
    keys_ref,
    weight_ref,
    bias_ref,
    keys_out,
    weight_out,
    bias_out,
    keys_buf,
    weight_buf,
    bias_buf,
    chunk_buf,
    full_buf,
    keys_send,
    keys_recv,
    weight_send,
    weight_recv,
    bias_send,
    bias_recv,
    full_send,
    full_recv,
):
    g = lax.axis_index("grp")
    t = lax.axis_index("tp")
    own = keys_out.shape[0]
    chunk = chunk_buf.shape[0]

    barrier = pltpu.get_barrier_semaphore()
    for d in range(1, n_grp):
        pl.semaphore_signal(barrier, inc=1, device_id={"grp": lax.rem(g + d, n_grp)})
    for d in range(1, n_tp):
        pl.semaphore_signal(barrier, inc=1, device_id={"tp": lax.rem(t + d, n_tp)})
    pl.semaphore_wait(barrier, n_grp + n_tp - 2)

    def rows_of(index, size):
        return pl.ds(pl.multiple_of(index * size, size), size)

    keys_copies, weight_copies, bias_copies, full_copies = [], [], [], []
    for d in range(1, n_grp):
        peer = lax.rem(g + d, n_grp)
        copy = pltpu.make_async_remote_copy(
            src_ref=weight_ref.at[rows_of(peer, chunk)],
            dst_ref=weight_buf.at[d - 1],
            send_sem=weight_send.at[d - 1],
            recv_sem=weight_recv.at[d - 1],
            device_id={"grp": peer},
        )
        copy.start()
        weight_copies.append(copy)
    for d in range(n_tp - 1, 0, -1):
        peer = lax.rem(t + d, n_tp)
        copy = pltpu.make_async_remote_copy(
            src_ref=keys_ref.at[rows_of(peer, own)],
            dst_ref=keys_buf.at[d - 1],
            send_sem=keys_send.at[d - 1],
            recv_sem=keys_recv.at[d - 1],
            device_id={"tp": peer},
        )
        copy.start()
        keys_copies.append(copy)
    for d in range(1, n_grp):
        copy = pltpu.make_async_remote_copy(
            src_ref=bias_ref,
            dst_ref=bias_buf.at[d - 1],
            send_sem=bias_send.at[d - 1],
            recv_sem=bias_recv.at[d - 1],
            device_id={"grp": lax.rem(g + d, n_grp)},
        )
        copy.start()
        bias_copies.append(copy)

    for copy in weight_copies:
        copy.wait()
    total = weight_ref[rows_of(g, chunk)].astype(F32)
    for d in range(n_grp - 1):
        total = total + weight_buf[d].astype(F32)
    chunk_buf[...] = total.astype(BF16)
    for d in range(1, n_grp):
        copy = pltpu.make_async_remote_copy(
            src_ref=chunk_buf,
            dst_ref=full_buf.at[g],
            send_sem=full_send.at[d - 1],
            recv_sem=full_recv.at[d - 1],
            device_id={"grp": lax.rem(g + d, n_grp)},
        )
        copy.start()
        full_copies.append(copy)
    full_buf[g] = chunk_buf[...]

    for copy in bias_copies:
        copy.wait()
    total = bias_ref[...]
    for d in range(n_grp - 1):
        total = total + bias_buf[d]
    bias_out[...] = total

    for copy in keys_copies:
        copy.wait()
    total = keys_ref[rows_of(t, own)].astype(F32)
    for d in range(n_tp - 1):
        total = total + keys_buf[d].astype(F32)
    keys_out[...] = total

    for copy in full_copies:
        copy.wait()
    weight_out[...] = full_buf[...].reshape(weight_out.shape)


def reduce_all(n_grp, n_tp, keys, weight, bias):
    own = keys.shape[0] // n_tp
    chunk = weight.shape[0] // n_grp
    columns = keys.shape[1]
    vmem = pl.BlockSpec(memory_space=pltpu.VMEM)
    dma = pltpu.SemaphoreType.DMA
    return pl.pallas_call(
        functools.partial(reduce_kernel, n_grp, n_tp),
        out_shape=(
            jax.ShapeDtypeStruct((own, columns), F32),
            jax.ShapeDtypeStruct(weight.shape, BF16),
            jax.ShapeDtypeStruct(bias.shape, F32),
        ),
        in_specs=[vmem] * 3,
        out_specs=(vmem,) * 3,
        scratch_shapes=[
            pltpu.VMEM((n_tp - 1, own, columns), BF16),
            pltpu.VMEM((n_grp - 1, chunk, columns), BF16),
            pltpu.VMEM((n_grp - 1,) + bias.shape, F32),
            pltpu.VMEM((chunk, columns), BF16),
            pltpu.VMEM((n_grp, chunk, columns), BF16),
            dma((n_tp - 1,)),
            dma((n_tp - 1,)),
            dma((n_grp - 1,)),
            dma((n_grp - 1,)),
            dma((n_grp - 1,)),
            dma((n_grp - 1,)),
            dma((n_grp - 1,)),
            dma((n_grp - 1,)),
        ],
        compiler_params=pltpu.CompilerParams(
            collective_id=0, has_side_effects=True, vmem_limit_bytes=32 * 1024 * 1024
        ),
    )(keys, weight, bias)


def on_device(
    text_embeds,
    image_embeds,
    image_offsets,
    image_counts,
    seq_lengths,
    norm_gain,
    key_weight,
    key_bias,
    key_cotangent,
):
    n_tp = lax.axis_size("tp")
    me = lax.axis_index("tp")
    rows = text_embeds.shape[0]
    width = image_embeds.shape[1]
    seqs, slots = image_offsets.shape
    length = rows // seqs
    own_image = image_embeds.shape[0]
    image_total = own_image * n_tp
    patch = image_total // (seqs * slots)
    own_count = key_cotangent.shape[0]

    position = lax.broadcasted_iota(jnp.int32, (seqs, length), 1)
    row_valid = (position < seq_lengths[:, None]).astype(F32).reshape(rows)
    own_valid = lax.dynamic_slice_in_dim(row_valid, me * own_count, own_count, 0)
    own_grad = lax.optimization_barrier(
        (key_cotangent.astype(F32) * own_valid[:, None]).astype(BF16)
    )

    text32 = text_embeds.astype(F32)
    image32 = image_embeds.astype(F32)
    own_squares = jnp.concatenate(
        [jnp.sum(text32 * text32, axis=1), jnp.sum(image32 * image32, axis=1)]
    )
    high = lax.reduce_precision(own_squares, 8, 7)
    rest = own_squares - high
    middle = lax.reduce_precision(rest, 8, 7)
    terms = jnp.concatenate([high, middle, rest - middle]).astype(BF16)
    columns = own_grad.shape[1]
    count = own_squares.shape[0]
    extra = -(-3 * count // (16 * columns)) * 16
    terms = jnp.pad(terms, (0, extra * columns - 3 * count)).reshape(extra, columns)
    gathered = lax.all_gather(jnp.concatenate([own_grad, terms], axis=0), "tp")
    masked_grad = gathered[:, :own_count].reshape(rows, columns)
    terms = gathered[:, own_count:].reshape(n_tp, extra * columns)[:, : 3 * count]
    parts = jnp.sum(terms.astype(F32).reshape(n_tp, 3, count), axis=1)
    squares = jnp.concatenate(
        [jnp.sum(parts[:, :rows], axis=0), parts[:, rows:].reshape(image_total)]
    )
    image_rows = lax.all_to_all(image_embeds, "tp", split_axis=1, concat_axis=0, tiled=True)
    image_rows = with_layout_constraint(image_rows, Layout((0, 1)))
    rstd = lax.rsqrt(squares / width + EPS)

    slot_used = lax.broadcasted_iota(jnp.int32, (seqs, slots), 1) < image_counts[:, None]
    inside = jnp.zeros((seqs, length), jnp.bool_)
    source = jnp.zeros((seqs, length), jnp.int32)
    first = lax.broadcasted_iota(jnp.int32, (seqs, length), 0) * (slots * patch)
    for k in range(slots):
        start = image_offsets[:, k : k + 1]
        here = slot_used[:, k : k + 1] & (position >= start) & (position < start + patch)
        source = jnp.where(here, first + k * patch + position - start, source)
        inside = inside | here
    text_rstd = rstd[:rows] * (1.0 - inside.astype(F32).reshape(rows))
    image_rstd = rstd[rows:]
    used = jnp.repeat(slot_used.reshape(-1).astype(F32), patch)

    gain32 = norm_gain.astype(F32)
    scaled_weight = (key_weight.astype(F32) * gain32[:, None]).astype(BF16)
    partial = (
        jnp.dot(text_embeds, scaled_weight, preferred_element_type=F32) * text_rstd[:, None]
    ).astype(BF16)
    text_grad = (masked_grad.astype(F32) * text_rstd[:, None]).astype(BF16)
    slot_starts = (
        lax.broadcasted_iota(jnp.int32, (seqs, slots), 0) * length + image_offsets
    ).reshape(-1)
    image_at = (
        slot_starts[:, None] + lax.broadcasted_iota(jnp.int32, (seqs * slots, patch), 1)
    ).reshape(-1)
    picked = jnp.take(masked_grad, image_at, axis=0, mode="clip")
    image_grad = (picked.astype(F32) * (image_rstd * used)[:, None]).astype(BF16)
    over_rows = (((0,), (0,)), ((), ()))
    text_part = lax.dot_general(text_embeds, text_grad, over_rows, preferred_element_type=F32)

    chosen = jnp.where(inside, source, -1).reshape(rows)
    place = (
        chosen[:, None] == lax.broadcasted_iota(jnp.int32, (rows, image_total), 1)
    ).astype(BF16)
    image_rows, partial, text_part, image_grad, place = lax.optimization_barrier(
        (image_rows, partial, text_part, image_grad, place)
    )
    image_keys = (
        jnp.dot(image_rows, scaled_weight, preferred_element_type=F32) * image_rstd[:, None]
    ).astype(BF16)
    placed = jnp.dot(place, image_keys, preferred_element_type=F32)
    partial = (partial.astype(F32) + placed).astype(BF16)
    image_part = lax.dot_general(image_rows, image_grad, over_rows, preferred_element_type=F32)
    weight_part = (text_part + image_part).astype(BF16)
    bias_part = jnp.sum(masked_grad.astype(F32).reshape(rows // 8, 8, -1), axis=0)
    n_grp = lax.axis_size("grp")
    if weight_part.shape[0] % (n_grp * 16) == 0 and own_count % 16 == 0:
        projected, total, bias_sum = reduce_all(n_grp, n_tp, partial, weight_part, bias_part)
    else:
        projected = lax.psum_scatter(partial, "tp", scatter_dimension=0, tiled=True)
        total = lax.psum(weight_part, "grp")
        bias_sum = lax.psum(bias_part, "grp")
    key_states = (
        (projected.astype(F32) + key_bias.astype(F32)[None, :]) * own_valid[:, None]
    ).astype(BF16)
    bias_grad = jnp.sum(bias_sum, axis=0)
    total = total.astype(F32)
    weight_grad = total * gain32[:, None]
    gain_grad = jnp.sum(total * key_weight.astype(F32), axis=1)
    return (key_states, weight_grad, bias_grad, gain_grad)


def solution(mesh):
    placed = (
        P("grp", "tp"),
        P(("grp", "tp"), None),
        P("grp", None),
        P("grp"),
        P("grp"),
        P("tp"),
        P("tp", None),
        P(),
        P(("grp", "tp"), None),
    )
    return jax.shard_map(
        on_device,
        mesh=mesh,
        in_specs=placed,
        out_specs=(P(("grp", "tp"), None), P("tp", None), P(), P("tp")),
        check_vma=False,
    )
```

```python
import functools

import jax
import jax.numpy as jnp
from jax import lax
from jax.experimental import pallas as pl
from jax.experimental.pallas import tpu as pltpu
from jax.experimental.layout import Layout, with_layout_constraint
from jax.sharding import PartitionSpec as P

EPS = 1e-06
F32 = jnp.float32
BF16 = jnp.bfloat16


def reduce_kernel(
    n_grp,
    n_tp,
    keys_ref,
    weight_ref,
    bias_ref,
    keys_out,
    weight_out,
    bias_out,
    keys_buf,
    weight_buf,
    bias_buf,
    chunk_buf,
    full_buf,
    keys_send,
    keys_recv,
    weight_send,
    weight_recv,
    bias_send,
    bias_recv,
    full_send,
    full_recv,
):
    g = lax.axis_index("grp")
    t = lax.axis_index("tp")
    own = keys_out.shape[0]
    chunk = chunk_buf.shape[0]

    barrier = pltpu.get_barrier_semaphore()
    for d in range(1, n_grp):
        pl.semaphore_signal(barrier, inc=1, device_id={"grp": lax.rem(g + d, n_grp)})
    for d in range(1, n_tp):
        pl.semaphore_signal(barrier, inc=1, device_id={"tp": lax.rem(t + d, n_tp)})
    pl.semaphore_wait(barrier, n_grp + n_tp - 2)

    def rows_of(index, size):
        return pl.ds(pl.multiple_of(index * size, size), size)

    keys_copies, weight_copies, bias_copies, full_copies = [], [], [], []
    for d in range(1, n_grp):
        peer = lax.rem(g + d, n_grp)
        copy = pltpu.make_async_remote_copy(
            src_ref=weight_ref.at[rows_of(peer, chunk)],
            dst_ref=weight_buf.at[d - 1],
            send_sem=weight_send.at[d - 1],
            recv_sem=weight_recv.at[d - 1],
            device_id={"grp": peer},
        )
        copy.start()
        weight_copies.append(copy)
    for d in range(n_tp - 1, 0, -1):
        peer = lax.rem(t + d, n_tp)
        copy = pltpu.make_async_remote_copy(
            src_ref=keys_ref.at[rows_of(peer, own)],
            dst_ref=keys_buf.at[d - 1],
            send_sem=keys_send.at[d - 1],
            recv_sem=keys_recv.at[d - 1],
            device_id={"tp": peer},
        )
        copy.start()
        keys_copies.append(copy)
    for d in range(1, n_grp):
        copy = pltpu.make_async_remote_copy(
            src_ref=bias_ref,
            dst_ref=bias_buf.at[d - 1],
            send_sem=bias_send.at[d - 1],
            recv_sem=bias_recv.at[d - 1],
            device_id={"grp": lax.rem(g + d, n_grp)},
        )
        copy.start()
        bias_copies.append(copy)

    for copy in weight_copies:
        copy.wait()
    total = weight_ref[rows_of(g, chunk)].astype(F32)
    for d in range(n_grp - 1):
        total = total + weight_buf[d].astype(F32)
    chunk_buf[...] = total.astype(BF16)
    for d in range(1, n_grp):
        copy = pltpu.make_async_remote_copy(
            src_ref=chunk_buf,
            dst_ref=full_buf.at[g],
            send_sem=full_send.at[d - 1],
            recv_sem=full_recv.at[d - 1],
            device_id={"grp": lax.rem(g + d, n_grp)},
        )
        copy.start()
        full_copies.append(copy)
    full_buf[g] = chunk_buf[...]

    for copy in bias_copies:
        copy.wait()
    total = bias_ref[...]
    for d in range(n_grp - 1):
        total = total + bias_buf[d]
    bias_out[...] = total

    for copy in keys_copies:
        copy.wait()
    total = keys_ref[rows_of(t, own)].astype(F32)
    for d in range(n_tp - 1):
        total = total + keys_buf[d].astype(F32)
    keys_out[...] = total

    for copy in full_copies:
        copy.wait()
    weight_out[...] = full_buf[...].reshape(weight_out.shape)


def reduce_all(n_grp, n_tp, keys, weight, bias):
    own = keys.shape[0] // n_tp
    chunk = weight.shape[0] // n_grp
    columns = keys.shape[1]
    vmem = pl.BlockSpec(memory_space=pltpu.VMEM)
    dma = pltpu.SemaphoreType.DMA
    return pl.pallas_call(
        functools.partial(reduce_kernel, n_grp, n_tp),
        out_shape=(
            jax.ShapeDtypeStruct((own, columns), F32),
            jax.ShapeDtypeStruct(weight.shape, BF16),
            jax.ShapeDtypeStruct(bias.shape, F32),
        ),
        in_specs=[vmem] * 3,
        out_specs=(vmem,) * 3,
        scratch_shapes=[
            pltpu.VMEM((n_tp - 1, own, columns), BF16),
            pltpu.VMEM((n_grp - 1, chunk, columns), BF16),
            pltpu.VMEM((n_grp - 1,) + bias.shape, F32),
            pltpu.VMEM((chunk, columns), BF16),
            pltpu.VMEM((n_grp, chunk, columns), BF16),
            dma((n_tp - 1,)),
            dma((n_tp - 1,)),
            dma((n_grp - 1,)),
            dma((n_grp - 1,)),
            dma((n_grp - 1,)),
            dma((n_grp - 1,)),
            dma((n_grp - 1,)),
            dma((n_grp - 1,)),
        ],
        compiler_params=pltpu.CompilerParams(
            collective_id=0, has_side_effects=True, vmem_limit_bytes=32 * 1024 * 1024
        ),
    )(keys, weight, bias)


def relay_kernel(
    n_tp, pieces, own_ref, out_ref, held, right_send, right_recv, left_send, left_recv
):
    t = lax.axis_index("tp")
    size = own_ref.shape[0] // pieces
    last = n_tp - 1

    barrier = pltpu.get_barrier_semaphore()

    for d in range(1, n_tp):
        pl.semaphore_signal(barrier, inc=1, device_id={"tp": lax.rem(t + d, n_tp)})
    pl.semaphore_wait(barrier, n_tp - 1)

    def move(step, piece, to_right):
        rows = pl.ds(piece * size, size)
        block = t - step if to_right else t + step
        block = jnp.clip(block, 0, last)
        source = own_ref.at[rows] if step == 0 else held.at[block, rows]
        send, recv = (right_send, right_recv) if to_right else (left_send, left_recv)
        peer = jnp.minimum(t + 1, last) if to_right else jnp.maximum(t - 1, 0)
        return pltpu.make_async_remote_copy(
            src_ref=source,
            dst_ref=held.at[block, rows],
            send_sem=send.at[step, piece],
            recv_sem=recv.at[step, piece],
            device_id={"tp": peer},
        )

    def sends(step, to_right):
        if to_right:
            return (t < last) & (t >= step)
        return (t > 0) & (t + step <= last)

    def receives(step, to_right):
        return t >= step + 1 if to_right else t + step + 1 <= last

    for step in range(n_tp - 1):
        for piece in range(pieces):
            for to_right in (True, False):
                if step > 0:

                    @pl.when(receives(step - 1, to_right))
                    def _():
                        move(step - 1, piece, to_right).wait_recv()

                @pl.when(sends(step, to_right))
                def _():
                    move(step, piece, to_right).start()

    for piece in range(pieces):
        for to_right in (True, False):

            @pl.when(receives(n_tp - 2, to_right))
            def _():
                move(n_tp - 2, piece, to_right).wait_recv()

    for step in range(n_tp - 1):
        for piece in range(pieces):
            for to_right in (True, False):

                @pl.when(sends(step, to_right))
                def _():
                    move(step, piece, to_right).wait_send()

    held[t] = own_ref[...]
    out_ref[...] = held[...]


def relay_gather(n_tp, own):
    pieces = 3 if own.shape[0] % 48 == 0 else 1
    vmem = pl.BlockSpec(memory_space=pltpu.VMEM)
    full = (n_tp,) + own.shape
    return pl.pallas_call(
        functools.partial(relay_kernel, n_tp, pieces),
        out_shape=jax.ShapeDtypeStruct(full, own.dtype),
        in_specs=[vmem],
        out_specs=vmem,
        scratch_shapes=[pltpu.VMEM(full, own.dtype)]
        + [pltpu.SemaphoreType.DMA((n_tp - 1, pieces))] * 4,
        compiler_params=pltpu.CompilerParams(
            collective_id=1, has_side_effects=True, vmem_limit_bytes=16 * 1024 * 1024
        ),
    )(own)


def on_device(
    text_embeds,
    image_embeds,
    image_offsets,
    image_counts,
    seq_lengths,
    norm_gain,
    key_weight,
    key_bias,
    key_cotangent,
):
    n_tp = lax.axis_size("tp")
    me = lax.axis_index("tp")
    rows = text_embeds.shape[0]
    width = image_embeds.shape[1]
    seqs, slots = image_offsets.shape
    length = rows // seqs
    own_image = image_embeds.shape[0]
    image_total = own_image * n_tp
    patch = image_total // (seqs * slots)
    own_count = key_cotangent.shape[0]

    position = lax.broadcasted_iota(jnp.int32, (seqs, length), 1)
    row_valid = (position < seq_lengths[:, None]).astype(F32).reshape(rows)
    own_valid = lax.dynamic_slice_in_dim(row_valid, me * own_count, own_count, 0)
    own_grad = lax.optimization_barrier(
        (key_cotangent.astype(F32) * own_valid[:, None]).astype(BF16)
    )

    text32 = text_embeds.astype(F32)
    image32 = image_embeds.astype(F32)
    own_squares = jnp.concatenate(
        [jnp.sum(text32 * text32, axis=1), jnp.sum(image32 * image32, axis=1)]
    )
    high = lax.reduce_precision(own_squares, 8, 7)
    rest = own_squares - high
    middle = lax.reduce_precision(rest, 8, 7)
    terms = jnp.concatenate([high, middle, rest - middle]).astype(BF16)
    columns = own_grad.shape[1]
    count = own_squares.shape[0]
    extra = -(-3 * count // (16 * columns)) * 16
    terms = jnp.pad(terms, (0, extra * columns - 3 * count)).reshape(extra, columns)
    gathered = relay_gather(n_tp, jnp.concatenate([own_grad, terms], axis=0))
    gathered, image_embeds = lax.optimization_barrier((gathered, image_embeds))
    masked_grad = gathered[:, :own_count].reshape(rows, columns)
    terms = gathered[:, own_count:].reshape(n_tp, extra * columns)[:, : 3 * count]
    parts = jnp.sum(terms.astype(F32).reshape(n_tp, 3, count), axis=1)
    squares = jnp.concatenate(
        [jnp.sum(parts[:, :rows], axis=0), parts[:, rows:].reshape(image_total)]
    )
    image_rows = lax.all_to_all(image_embeds, "tp", split_axis=1, concat_axis=0, tiled=True)
    image_rows = with_layout_constraint(image_rows, Layout((0, 1)))
    rstd = lax.rsqrt(squares / width + EPS)

    slot_used = lax.broadcasted_iota(jnp.int32, (seqs, slots), 1) < image_counts[:, None]
    inside = jnp.zeros((seqs, length), jnp.bool_)
    source = jnp.zeros((seqs, length), jnp.int32)
    first = lax.broadcasted_iota(jnp.int32, (seqs, length), 0) * (slots * patch)
    for k in range(slots):
        start = image_offsets[:, k : k + 1]
        here = slot_used[:, k : k + 1] & (position >= start) & (position < start + patch)
        source = jnp.where(here, first + k * patch + position - start, source)
        inside = inside | here
    text_rstd = rstd[:rows] * (1.0 - inside.astype(F32).reshape(rows))
    image_rstd = rstd[rows:]
    used = jnp.repeat(slot_used.reshape(-1).astype(F32), patch)

    gain32 = norm_gain.astype(F32)
    scaled_weight = (key_weight.astype(F32) * gain32[:, None]).astype(BF16)
    partial = (
        jnp.dot(text_embeds, scaled_weight, preferred_element_type=F32) * text_rstd[:, None]
    ).astype(BF16)
    text_grad = (masked_grad.astype(F32) * text_rstd[:, None]).astype(BF16)
    slot_starts = (
        lax.broadcasted_iota(jnp.int32, (seqs, slots), 0) * length + image_offsets
    ).reshape(-1)
    image_at = (
        slot_starts[:, None] + lax.broadcasted_iota(jnp.int32, (seqs * slots, patch), 1)
    ).reshape(-1)
    picked = jnp.take(masked_grad, image_at, axis=0, mode="clip")
    image_grad = (picked.astype(F32) * (image_rstd * used)[:, None]).astype(BF16)
    over_rows = (((0,), (0,)), ((), ()))
    text_part = lax.dot_general(text_embeds, text_grad, over_rows, preferred_element_type=F32)

    chosen = jnp.where(inside, source, -1).reshape(rows)
    place = (
        chosen[:, None] == lax.broadcasted_iota(jnp.int32, (rows, image_total), 1)
    ).astype(BF16)
    image_rows, partial, text_part, image_grad, place = lax.optimization_barrier(
        (image_rows, partial, text_part, image_grad, place)
    )
    image_keys = (
        jnp.dot(image_rows, scaled_weight, preferred_element_type=F32) * image_rstd[:, None]
    ).astype(BF16)
    placed = jnp.dot(place, image_keys, preferred_element_type=F32)
    partial = (partial.astype(F32) + placed).astype(BF16)
    image_part = lax.dot_general(image_rows, image_grad, over_rows, preferred_element_type=F32)
    weight_part = (text_part + image_part).astype(BF16)
    bias_part = jnp.sum(masked_grad.astype(F32).reshape(rows // 8, 8, -1), axis=0)
    n_grp = lax.axis_size("grp")
    if weight_part.shape[0] % (n_grp * 16) == 0 and own_count % 16 == 0:
        projected, total, bias_sum = reduce_all(n_grp, n_tp, partial, weight_part, bias_part)
    else:
        projected = lax.psum_scatter(partial, "tp", scatter_dimension=0, tiled=True)
        total = lax.psum(weight_part, "grp")
        bias_sum = lax.psum(bias_part, "grp")
    key_states = (
        (projected.astype(F32) + key_bias.astype(F32)[None, :]) * own_valid[:, None]
    ).astype(BF16)
    bias_grad = jnp.sum(bias_sum, axis=0)
    total = total.astype(F32)
    weight_grad = total * gain32[:, None]
    gain_grad = jnp.sum(total * key_weight.astype(F32), axis=1)
    return (key_states, weight_grad, bias_grad, gain_grad)


def solution(mesh):
    placed = (
        P("grp", "tp"),
        P(("grp", "tp"), None),
        P("grp", None),
        P("grp"),
        P("grp"),
        P("tp"),
        P("tp", None),
        P(),
        P(("grp", "tp"), None),
    )
    return jax.shard_map(
        on_device,
        mesh=mesh,
        in_specs=placed,
        out_specs=(P(("grp", "tp"), None), P("tp", None), P(), P("tp")),
        check_vma=False,
    )
```
